32 devices in a mesh: grp: 2 (over y), frame: 4 (over x, core), band: 4 (over z).
Axes of the slice: x: 2, y: 2, z: 4, core: 2. Of those that a mesh axis runs over, the one named last changes fastest.
Arguments:
- features: bfloat16 [16, 64, 128, 256], P(('grp', 'frame'), 'band'), parts along dimension 0, may hold values from -6 to 6
- space_kernel: bfloat16 [3, 3, 256, 256], replicated, may hold values from -0.125 to 0.125
- space_gain: float32 [256], replicated, may hold values from 0.5 to 2
- space_bias: float32 [256], replicated, may hold values from -3 to 3
- time_kernel: bfloat16 [3, 256, 256], replicated, may hold values from -0.21875 to 0.21875
- time_gain: float32 [256], replicated, may hold values from 0.5 to 2
- time_bias: float32 [256], replicated, may hold values from -3 to 3
Outputs:
- decoded: bfloat16 [16, 64, 128, 256], P(('grp', 'frame'), 'band'), parts along dimension 0
The draws below stay inside these ranges and needn't reach their ends.
There are 2 independent parts, one for each index of `grp`. The reference program is written for one: setup_inputs(seed, part) draws one part's arguments, and reference() takes and returns one part's arrays. A program takes and returns all parts, laid end to end along the dimension named above; an argument that names none is the same for every part. Nothing has to cross between parts.
All inputs are finite; a program needn't handle non-finite values.
Results may differ from the reference program's by a relative error of at most 0.0056.
Values may be sent and summed in bfloat16 or wider, within the bound.
A program may use at most 64 MiB of HBM per device.

```python
import math
import jax
import jax.numpy as jnp
from jax import lax

C = 256
W = 128
F = 8
H = 64


def block_scale(rng, shape, split, low, high):
    factor_of, own = 1.0, jax.random.fold_in(rng, 6)
    for dim, shards_of in split:
        heights = jnp.exp(jax.random.uniform(jax.random.fold_in(own, dim), (shards_of,), jnp.float32, low / len(split), high / len(split)))
        factor_of = factor_of * jnp.repeat(heights, shape[dim] // shards_of).reshape([-1 if axis == dim else 1 for axis in range(len(shape))])
    return factor_of


def bell_draw(key, shape, scale, limit, shards=(), kind=jnp.bfloat16):
    entries = jax.random.normal(key, shape, jnp.float32) * scale
    if len(shards) > 0:
        entries = block_scale(key, shape, shards, -0.22, 0.18) * entries
    return jnp.clip(entries, min=-limit, max=limit).astype(kind)


def setup_inputs(seed: int = 0, part: int = 0) -> dict:
    keys = jax.random.split(jax.random.key(seed), 8)
    own_keys = jax.random.split(jax.random.fold_in(keys[7], part), 8)
    features = bell_draw(own_keys[0], (F, H, W, C), 1.0, 6.0, ((0, 4), (1, 4)))
    space_kernel = bell_draw(keys[1], (3, 3, C, C), (9 * C) ** -0.5, 0.125)
    space_gain = jnp.clip(jnp.exp(jax.random.uniform(keys[2], (C,), jnp.float32, math.log(0.5), math.log(2.0))), 0.5, 2.0)
    space_bias = bell_draw(keys[3], (C,), 0.5, 3.0, (), jnp.float32)
    time_kernel = bell_draw(keys[4], (3, C, C), (3 * C) ** -0.5, 0.21875)
    time_gain = jnp.clip(jnp.exp(jax.random.uniform(keys[5], (C,), jnp.float32, math.log(0.5), math.log(2.0))), 0.5, 2.0)
    time_bias = bell_draw(keys[6], (C,), 0.5, 3.0, (), jnp.float32)
    return {"features": features, "space_kernel": space_kernel, "space_gain": space_gain, "space_bias": space_bias, "time_kernel": time_kernel, "time_gain": time_gain, "time_bias": time_bias}


def rms_silu(values, gain_vector):
    widened = values.astype(jnp.float32)
    scaled = widened * lax.rsqrt(lax.optimization_barrier(jnp.mean(widened * widened, axis=-1, keepdims=True)) + 1e-06) * gain_vector
    return jax.nn.silu(scaled).astype(jnp.bfloat16)

def spatial_frame(normed_frame, kernel):
    rows_count, cols_count, channels = normed_frame.shape
    padded = jnp.pad(normed_frame, ((1, 1), (1, 1), (0, 0)))
    summed = jnp.zeros((rows_count * cols_count, kernel.shape[3]), jnp.float32)
    for tap_row in range(3):
        for tap_col in range(3):
            window = padded[tap_row:tap_row + rows_count, tap_col:tap_col + cols_count].reshape(-1, channels)
            summed = summed + jnp.dot(window, kernel[tap_row, tap_col], preferred_element_type=jnp.float32)
    return summed.reshape(rows_count, cols_count, -1)

def reference(features, space_kernel, space_gain, space_bias, time_kernel, time_gain, time_bias):
    normed = rms_silu(features, space_gain)
    spatial = lax.map(lambda frame_data: spatial_frame(frame_data, space_kernel), normed)
    hidden = (features.astype(jnp.float32) + spatial + space_bias).astype(jnp.bfloat16)
    hidden = lax.optimization_barrier(hidden)
    normed_time = rms_silu(hidden, time_gain)
    frame_count = normed_time.shape[0]
    channels = normed_time.shape[-1]
    extended = jnp.pad(normed_time, ((2, 0), (0, 0), (0, 0), (0, 0)))
    summed = jnp.zeros((normed_time.size // channels, channels), jnp.float32)
    for time_lag in range(3):
        window = extended[2 - time_lag:2 - time_lag + frame_count].reshape(-1, channels)
        summed = summed + jnp.dot(window, time_kernel[time_lag], preferred_element_type=jnp.float32)
    temporal = summed.reshape(normed_time.shape).astype(jnp.bfloat16)
    temporal = lax.optimization_barrier(temporal)
    decoded = hidden.astype(jnp.float32) + temporal.astype(jnp.float32) + time_bias
    return decoded.astype(jnp.bfloat16)
```

```python
import functools

import jax
import jax.numpy as jnp
from jax import lax
from jax.experimental import pallas as pl
from jax.experimental.pallas import tpu as pltpu
from jax.sharding import PartitionSpec as P

LAGS = 2


def rms_silu(values, gain):
    mean = jnp.mean(values * values, axis=-1, keepdims=True)
    scaled = values * lax.rsqrt(mean + 1e-06) * gain
    return scaled / (1.0 + jnp.exp(-scaled))


def kernel(
    features, space_kernel, space_gain, space_bias, time_kernel, time_gain, time_bias,
    out,
    feat, normed, hidden, ntime, earlier, wspace, wtime, vectors,
    feat_sem, weight_sem, halo_send, halo_recv, time_send, time_recv,
):
    frames, rows, cols, channels = features.shape
    pixels = frames * cols
    band, bands = lax.axis_index("band"), lax.axis_size("band")
    frame, frame_parts = lax.axis_index("frame"), lax.axis_size("frame")
    has_up, has_down = band > 0, band < bands - 1
    has_prev, has_next = frame > 0, frame < frame_parts - 1
    neighbours = (
        (has_up, {"band": band - 1}),
        (has_down, {"band": band + 1}),
        (has_prev, {"frame": frame - 1}),
        (has_next, {"frame": frame + 1}),
    )

    barrier = pltpu.get_barrier_semaphore()
    for present, device in neighbours:
        @pl.when(present)
        def _():
            pl.semaphore_signal(
                barrier, inc=1, device_id=device, device_id_type=pl.DeviceIdType.MESH
            )

    def row_copy(row):
        return pltpu.make_async_copy(
            features.at[:, row], feat.at[row + 1], feat_sem.at[row]
        )

    weights = [(space_kernel, wspace), (time_kernel, wtime)] + [
        (vector, vectors.at[i])
        for i, vector in enumerate((space_gain, space_bias, time_gain, time_bias))
    ]
    weight_copies = [
        pltpu.make_async_copy(source, target, weight_sem.at[i])
        for i, (source, target) in enumerate(weights)
    ]
    for i in (2, 3, 4, 5):
        weight_copies[i].start()
    for row in range(min(3, rows)):
        row_copy(row).start()
    weight_copies[0].start()
    for row in range(3, rows):
        row_copy(row).start()
    weight_copies[1].start()

    peers = (
        (band + bands - 1) // bands
        + 1 - (band + 1) // bands
        + (frame + frame_parts - 1) // frame_parts
        + 1 - (frame + 1) // frame_parts
    )
    pl.semaphore_wait(barrier, peers)

    to_up = pltpu.make_async_remote_copy(
        features.at[:, 0], feat.at[rows + 1], halo_send.at[0], halo_recv.at[0],
        device_id={"band": band - 1}, device_id_type=pl.DeviceIdType.MESH,
    )
    to_down = pltpu.make_async_remote_copy(
        features.at[:, rows - 1], feat.at[0], halo_send.at[1], halo_recv.at[1],
        device_id={"band": band + 1}, device_id_type=pl.DeviceIdType.MESH,
    )
    pl.when(has_up)(to_up.start)
    pl.when(has_down)(to_down.start)

    def time_copy(row):
        return pltpu.make_async_remote_copy(
            ntime.at[row, pl.ds(pixels - LAGS * cols, LAGS * cols)],
            earlier.at[row],
            time_send.at[row],
            time_recv.at[row],
            device_id={"frame": frame + 1},
            device_id_type=pl.DeviceIdType.MESH,
        )

    column = lax.rem(lax.broadcasted_iota(jnp.int32, (pixels, channels), 0), cols)

    def vector(i):
        return vectors[i].reshape(1, channels)

    def norm_row(slot):
        values = feat[slot].reshape(pixels, channels).astype(jnp.float32)
        result = rms_silu(values, vector(0))
        left = jnp.where(column == 0, 0.0, pltpu.roll(result, 1, 0))
        right = jnp.where(column == cols - 1, 0.0, pltpu.roll(result, pixels - 1, 0))
        normed[slot, :, :channels] = left.astype(jnp.bfloat16)
        normed[slot, :, channels : 2 * channels] = result.astype(jnp.bfloat16)
        normed[slot, :, 2 * channels :] = right.astype(jnp.bfloat16)

    def space_row(row):
        total = None
        for i in range(3):
            product = jnp.dot(
                normed[row + i],
                wspace[i].reshape(3 * channels, channels),
                preferred_element_type=jnp.float32,
            )
            total = product if total is None else total + product
        centre = feat[row + 1].reshape(pixels, channels).astype(jnp.float32)
        kept = (centre + total + vector(1)).astype(jnp.bfloat16)
        hidden[row] = kept
        ntime[row] = rms_silu(kept.astype(jnp.float32), vector(2)).astype(jnp.bfloat16)

        @pl.when(has_next)
        def _():
            time_copy(row).start()

    def time_row(row):
        pl.when(has_prev)(time_copy(row).wait_recv)
        own = ntime[row]
        window = jnp.concatenate([earlier[row], own], axis=0)
        total = jnp.dot(own, wtime[0], preferred_element_type=jnp.float32)
        for lag in range(1, LAGS + 1):
            start = (LAGS - lag) * cols
            total = total + jnp.dot(
                window[start : start + pixels], wtime[lag],
                preferred_element_type=jnp.float32,
            )
        temporal = total.astype(jnp.bfloat16).astype(jnp.float32)
        decoded = hidden[row].astype(jnp.float32) + temporal + vector(3)
        out[:, row] = decoded.astype(jnp.bfloat16).reshape(frames, cols, channels)

    @pl.when(jnp.logical_not(has_prev))
    def _():
        earlier[...] = jnp.zeros_like(earlier)

    @pl.when(jnp.logical_not(has_up))
    def _():
        feat[0] = jnp.zeros(feat.shape[1:], feat.dtype)

    @pl.when(jnp.logical_not(has_down))
    def _():
        feat[rows + 1] = jnp.zeros(feat.shape[1:], feat.dtype)

    for i in (2, 3, 4, 5):
        weight_copies[i].wait()

    @pl.loop(0, 2)
    def _(row):
        row_copy(row).wait()
        norm_row(row + 1)

    row_copy(2).wait()
    norm_row(3)
    weight_copies[0].wait()
    space_row(1)

    @pl.loop(2, rows - 1)
    def _(row):
        row_copy(row + 1).wait()
        norm_row(row + 2)
        space_row(row)

    pl.when(has_up)(to_down.wait_recv)
    pl.when(has_down)(to_up.wait_recv)

    @pl.loop(0, 2)
    def _(side):
        norm_row(side * (rows + 1))
        space_row(side * (rows - 1))

    weight_copies[1].wait()

    @pl.loop(1, rows + 1)
    def _(step):
        time_row(order(step, rows))

    pl.when(has_up)(to_up.wait_send)
    pl.when(has_down)(to_down.wait_send)

    @pl.when(has_next)
    def _():
        @pl.loop(0, rows)
        def _(row):
            time_copy(row).wait_send()


def order(step, rows):
    late = step // (rows - 1)
    last = step // rows
    return step * (1 - late) + last * (rows - 1)


def body(features, *rest):
    frames, rows, cols, channels = features.shape
    pixels = frames * cols
    bf16 = jnp.bfloat16
    return pl.pallas_call(
        kernel,
        out_shape=jax.ShapeDtypeStruct(features.shape, bf16),
        in_specs=[pl.BlockSpec(memory_space=pltpu.HBM)] * 7,
        out_specs=pl.BlockSpec(memory_space=pltpu.VMEM),
        scratch_shapes=[
            pltpu.VMEM((rows + 2, frames, cols, channels), bf16),
            pltpu.VMEM((rows + 2, pixels, 3 * channels), bf16),
            pltpu.VMEM((rows, pixels, channels), bf16),
            pltpu.VMEM((rows, pixels, channels), bf16),
            pltpu.VMEM((rows, LAGS * cols, channels), bf16),
            pltpu.VMEM(rest[0].shape, bf16),
            pltpu.VMEM(rest[3].shape, bf16),
            pltpu.VMEM((4, channels), jnp.float32),
            pltpu.SemaphoreType.DMA((rows,)),
            pltpu.SemaphoreType.DMA((6,)),
            pltpu.SemaphoreType.DMA((2,)),
            pltpu.SemaphoreType.DMA((2,)),
            pltpu.SemaphoreType.DMA((rows,)),
            pltpu.SemaphoreType.DMA((rows,)),
        ],
        compiler_params=pltpu.CompilerParams(
            collective_id=0, has_side_effects=True, vmem_limit_bytes=36 * 1024 * 1024
        ),
    )(features, *rest)


def solution(mesh):
    return jax.shard_map(
        body,
        mesh=mesh,
        in_specs=(P(("grp", "frame"), "band", None, None), P(), P(), P(), P(), P(), P()),
        out_specs=P(("grp", "frame"), "band", None, None),
        check_vma=False,
    )
```

```python
import functools

import jax
import jax.numpy as jnp
from jax import lax
from jax.experimental import pallas as pl
from jax.experimental.pallas import tpu as pltpu
from jax.sharding import PartitionSpec as P

LAGS = 2


def rms_silu(values, gain):
    mean = jnp.mean(values * values, axis=-1, keepdims=True)
    scaled = values * lax.rsqrt(mean + 1e-06) * gain
    return scaled / (1.0 + jnp.exp(-scaled))


def kernel(
    features, space_kernel, space_gain, space_bias, time_kernel, time_gain, time_bias,
    out,
    feat, normed, hidden, ntime, earlier, wspace, wtime, vectors,
    feat_sem, weight_sem, halo_send, halo_recv, time_send, time_recv,
):
    frames, rows, cols, channels = features.shape
    pixels = frames * cols
    band, bands = lax.axis_index("band"), lax.axis_size("band")
    frame, frame_parts = lax.axis_index("frame"), lax.axis_size("frame")
    has_up, has_down = band > 0, band < bands - 1
    has_prev, has_next = frame > 0, frame < frame_parts - 1
    neighbours = (
        (has_up, {"band": band - 1}),
        (has_down, {"band": band + 1}),
        (has_prev, {"frame": frame - 1}),
        (has_next, {"frame": frame + 1}),
    )

    barrier = pltpu.get_barrier_semaphore()
    for present, device in neighbours:
        @pl.when(present)
        def _():
            pl.semaphore_signal(
                barrier, inc=1, device_id=device, device_id_type=pl.DeviceIdType.MESH
            )

    def row_copy(row):
        return pltpu.make_async_copy(
            features.at[:, row], feat.at[row + 1], feat_sem.at[row]
        )

    weights = [(space_kernel, wspace), (time_kernel, wtime)] + [
        (vector, vectors.at[i])
        for i, vector in enumerate((space_gain, space_bias, time_gain, time_bias))
    ]
    weight_copies = [
        pltpu.make_async_copy(source, target, weight_sem.at[i])
        for i, (source, target) in enumerate(weights)
    ]
    for i in (2, 3, 4, 5):
        weight_copies[i].start()
    for row in range(min(3, rows)):
        row_copy(row).start()
    weight_copies[0].start()
    for row in range(3, rows):
        row_copy(row).start()
    weight_copies[1].start()

    peers = (
        (band + bands - 1) // bands
        + 1 - (band + 1) // bands
        + (frame + frame_parts - 1) // frame_parts
        + 1 - (frame + 1) // frame_parts
    )
    pl.semaphore_wait(barrier, peers)

    to_up = pltpu.make_async_remote_copy(
        features.at[:, 0], feat.at[rows + 1], halo_send.at[0], halo_recv.at[0],
        device_id={"band": band - 1}, device_id_type=pl.DeviceIdType.MESH,
    )
    to_down = pltpu.make_async_remote_copy(
        features.at[:, rows - 1], feat.at[0], halo_send.at[1], halo_recv.at[1],
        device_id={"band": band + 1}, device_id_type=pl.DeviceIdType.MESH,
    )
    pl.when(has_up)(to_up.start)
    pl.when(has_down)(to_down.start)

    def time_copy(row):
        return pltpu.make_async_remote_copy(
            ntime.at[row, pl.ds(pixels - LAGS * cols, LAGS * cols)],
            earlier.at[row],
            time_send.at[row],
            time_recv.at[row],
            device_id={"frame": frame + 1},
            device_id_type=pl.DeviceIdType.MESH,
        )

    column = lax.rem(lax.broadcasted_iota(jnp.int32, (pixels, channels), 0), cols)

    def vector(i):
        return vectors[i].reshape(1, channels)

    def norm_row(slot):
        values = feat[slot].reshape(pixels, channels).astype(jnp.float32)
        result = rms_silu(values, vector(0))
        left = jnp.where(column == 0, 0.0, pltpu.roll(result, 1, 0))
        right = jnp.where(column == cols - 1, 0.0, pltpu.roll(result, pixels - 1, 0))
        normed[slot, :, :channels] = left.astype(jnp.bfloat16)
        normed[slot, :, channels : 2 * channels] = result.astype(jnp.bfloat16)
        normed[slot, :, 2 * channels :] = right.astype(jnp.bfloat16)

    def space_row(row):
        total = None
        for i in range(3):
            product = jnp.dot(
                normed[row + i],
                wspace[i].reshape(3 * channels, channels),
                preferred_element_type=jnp.float32,
            )
            total = product if total is None else total + product
        centre = feat[row + 1].reshape(pixels, channels).astype(jnp.float32)
        kept = (centre + total + vector(1)).astype(jnp.bfloat16)
        hidden[row] = kept
        ntime[row] = rms_silu(kept.astype(jnp.float32), vector(2)).astype(jnp.bfloat16)

        @pl.when(has_next)
        def _():
            time_copy(row).start()

    def time_row(row):
        pl.when(has_prev)(time_copy(row).wait_recv)
        own = ntime[row]
        window = jnp.concatenate([earlier[row], own], axis=0)
        total = jnp.dot(own, wtime[0], preferred_element_type=jnp.float32)
        for lag in range(1, LAGS + 1):
            start = (LAGS - lag) * cols
            total = total + jnp.dot(
                window[start : start + pixels], wtime[lag],
                preferred_element_type=jnp.float32,
            )
        temporal = total.astype(jnp.bfloat16).astype(jnp.float32)
        decoded = hidden[row].astype(jnp.float32) + temporal + vector(3)
        out[:, row] = decoded.astype(jnp.bfloat16).reshape(frames, cols, channels)

    @pl.when(jnp.logical_not(has_prev))
    def _():
        earlier[...] = jnp.zeros_like(earlier)

    @pl.when(jnp.logical_not(has_up))
    def _():
        feat[0] = jnp.zeros(feat.shape[1:], feat.dtype)

    @pl.when(jnp.logical_not(has_down))
    def _():
        feat[rows + 1] = jnp.zeros(feat.shape[1:], feat.dtype)

    for i in (2, 3, 4, 5):
        weight_copies[i].wait()

    @pl.loop(0, 2)
    def _(row):
        row_copy(row).wait()
        norm_row(row + 1)

    row_copy(2).wait()
    norm_row(3)
    weight_copies[0].wait()
    space_row(1)

    @pl.loop(2, rows - 1)
    def _(row):
        row_copy(row + 1).wait()
        norm_row(row + 2)
        space_row(row)

    pl.when(has_up)(to_down.wait_recv)
    pl.when(has_down)(to_up.wait_recv)

    @pl.loop(0, 2)
    def _(side):
        norm_row(side * (rows + 1))
        space_row(side * (rows - 1))

    weight_copies[1].wait()

    @pl.loop(1, rows + 1)
    def _(step):
        time_row(order(step, rows))

    pl.when(has_up)(to_up.wait_send)
    pl.when(has_down)(to_down.wait_send)

    @pl.when(has_next)
    def _():
        @pl.loop(0, rows)
        def _(row):
            time_copy(row).wait_send()


def order(step, rows):
    late = step // (rows - 1)
    last = step // rows
    return step * (1 - late) + last * (rows - 1)


def body(features, *rest):
    frames, rows, cols, channels = features.shape
    pixels = frames * cols
    bf16 = jnp.bfloat16
    return pl.pallas_call(
        kernel,
        out_shape=jax.ShapeDtypeStruct(features.shape, bf16),
        in_specs=[pl.BlockSpec(memory_space=pltpu.HBM)] * 7,
        out_specs=pl.BlockSpec(memory_space=pltpu.VMEM),
        scratch_shapes=[
            pltpu.VMEM((rows + 2, frames, cols, channels), bf16),
            pltpu.VMEM((rows + 2, pixels, 3 * channels), bf16),
            pltpu.VMEM((rows, pixels, channels), bf16),
            pltpu.VMEM((rows, pixels, channels), bf16),
            pltpu.VMEM((rows, LAGS * cols, channels), bf16),
            pltpu.VMEM(rest[0].shape, bf16),
            pltpu.VMEM(rest[3].shape, bf16),
            pltpu.VMEM((4, channels), jnp.float32),
            pltpu.SemaphoreType.DMA((rows,)),
            pltpu.SemaphoreType.DMA((6,)),
            pltpu.SemaphoreType.DMA((2,)),
            pltpu.SemaphoreType.DMA((2,)),
            pltpu.SemaphoreType.DMA((rows,)),
            pltpu.SemaphoreType.DMA((rows,)),
        ],
        compiler_params=pltpu.CompilerParams(
            collective_id=0, has_side_effects=True, vmem_limit_bytes=36 * 1024 * 1024
        ),
    )(*[pltpu.with_memory_space_constraint(x, pltpu.HBM) for x in (features, *rest)])


def solution(mesh):
    return jax.shard_map(
        body,
        mesh=mesh,
        in_specs=(P(("grp", "frame"), "band", None, None), P(), P(), P(), P(), P(), P()),
        out_specs=P(("grp", "frame"), "band", None, None),
        check_vma=False,
    )
```

```python
import functools

import jax
import jax.numpy as jnp
from jax import lax
from jax.experimental import pallas as pl
from jax.experimental.pallas import tpu as pltpu
from jax.sharding import PartitionSpec as P

LAGS = 2


def rms_silu(values, gain):
    mean = jnp.mean(values * values, axis=-1, keepdims=True)
    half = values * lax.rsqrt(mean + 1e-06) * (0.5 * gain)
    return half + half * jnp.tanh(half)


def dot(left, right):
    return jnp.dot(left, right, preferred_element_type=jnp.float32)


def kernel(
    features, space_kernel, space_gain, space_bias, time_kernel, time_gain, time_bias,
    out,
    feat, normed, hidden, ntime, earlier, wspace, wtime, vectors,
    feat_sem, weight_sem, halo_send, halo_recv, time_send, time_recv,
):
    frames, rows, cols, channels = features.shape
    half = cols // 2
    first, last = 1, rows - 1
    band, bands = lax.axis_index("band"), lax.axis_size("band")
    frame, frame_parts = lax.axis_index("frame"), lax.axis_size("frame")
    has_up, has_down = band > 0, band < bands - 1
    has_prev, has_next = frame > 0, frame < frame_parts - 1
    neighbours = (
        (has_up, {"band": band - 1}),
        (has_down, {"band": band + 1}),
        (has_prev, {"frame": frame - 1}),
        (has_next, {"frame": frame + 1}),
    )

    barrier = pltpu.get_barrier_semaphore()
    for present, device in neighbours:
        @pl.when(present)
        def _():
            pl.semaphore_signal(
                barrier, inc=1, device_id=device, device_id_type=pl.DeviceIdType.MESH
            )

    def row_copy(row):
        return pltpu.make_async_copy(
            features.at[:, row], feat.at[row + 1], feat_sem.at[row]
        )

    weights = [(space_kernel, wspace), (time_kernel, wtime)] + [
        (vector, vectors.at[i])
        for i, vector in enumerate((space_gain, space_bias, time_gain, time_bias))
    ]
    weight_copies = [
        pltpu.make_async_copy(source, target, weight_sem.at[i])
        for i, (source, target) in enumerate(weights)
    ]
    for i in (2, 3, 4, 5):
        weight_copies[i].start()
    for row in range(3):
        row_copy(row).start()
    weight_copies[0].start()
    for row in range(3, rows):
        row_copy(row).start()
    weight_copies[1].start()

    peers = (
        (band + bands - 1) // bands
        + 1 - (band + 1) // bands
        + (frame + frame_parts - 1) // frame_parts
        + 1 - (frame + 1) // frame_parts
    )
    pl.semaphore_wait(barrier, peers)

    to_up = pltpu.make_async_remote_copy(
        features.at[:, 0], feat.at[rows + 1], halo_send.at[0], halo_recv.at[0],
        device_id={"band": band - 1}, device_id_type=pl.DeviceIdType.MESH,
    )
    to_down = pltpu.make_async_remote_copy(
        features.at[:, rows - 1], feat.at[0], halo_send.at[1], halo_recv.at[1],
        device_id={"band": band + 1}, device_id_type=pl.DeviceIdType.MESH,
    )
    pl.when(has_up)(to_up.start)
    pl.when(has_down)(to_down.start)

    def time_copy(row, sem, start=0, count=LAGS, left=0, width=cols):
        return pltpu.make_async_remote_copy(
            ntime.at[row, pl.ds(frames - LAGS + start, count), pl.ds(left, width)],
            earlier.at[row, pl.ds(start, count), pl.ds(left, width)],
            time_send.at[sem],
            time_recv.at[sem],
            device_id={"frame": frame + 1},
            device_id_type=pl.DeviceIdType.MESH,
        )

    first_copies = {
        (start, side): time_copy(first, rows + 2 * start + side, start, 1, side * half, half)
        for start in range(LAGS)
        for side in range(2)
    }
    last_copies = [
        time_copy(last, rows + 2 * LAGS + side, 0, LAGS, side * half, half)
        for side in range(2)
    ]

    def vector(i):
        return vectors[i].reshape(1, channels)

    def norm_part(slot, start=0, count=frames, left=0, width=cols):
        base = max(0, min(left - 16, cols - width - 16)) if width < cols else 0
        window = min(cols, width + 16)
        size = count * window
        values = feat[slot, start : start + count, base : base + window]
        result = rms_silu(values.reshape(size, channels).astype(jnp.float32), vector(0))
        column = base + lax.rem(
            lax.broadcasted_iota(jnp.int32, (size, channels), 0), window
        )
        before = jnp.where(column == 0, 0.0, pltpu.roll(result, 1, 0))
        after = jnp.where(column == cols - 1, 0.0, pltpu.roll(result, size - 1, 0))
        for i, piece in enumerate((before, result, after)):
            kept = piece.astype(jnp.bfloat16).reshape(count, window, channels)
            normed[
                slot, start : start + count, left : left + width,
                i * channels : (i + 1) * channels,
            ] = kept[:, left - base : left - base + width]

    def space_part(row, start=0, count=frames, left=0, width=cols):
        where = (slice(start, start + count), slice(left, left + width))
        size = count * width
        total = None
        for i in range(3):
            product = dot(
                normed[(row + i, *where)].reshape(size, 3 * channels),
                wspace[i].reshape(3 * channels, channels),
            )
            total = product if total is None else total + product
        centre = feat[(row + 1, *where)].reshape(size, channels).astype(jnp.float32)
        kept = (centre + total + vector(1)).astype(jnp.bfloat16)
        shape = (count, width, channels)
        hidden[(row, *where)] = kept.reshape(shape)
        ntime[(row, *where)] = (
            rms_silu(kept.astype(jnp.float32), vector(2)).astype(jnp.bfloat16).reshape(shape)
        )

    def space_row(row):
        space_part(row)
        pl.when(has_next)(time_copy(row, row).start)

    def time_part(row, copies, left=0, width=cols):
        columns = slice(left, left + width)
        own = ntime[row, :, columns]
        totals = [
            dot(own.reshape(-1, channels), wtime[0]).reshape(own.shape)[f]
            for f in range(frames)
        ]
        for lag in range(1, min(LAGS, frames - 1) + 1):
            term = dot(own[: frames - lag].reshape(-1, channels), wtime[lag])
            for f in range(lag, frames):
                totals[f] += term[(f - lag) * width : (f - lag + 1) * width]

        @pl.when(has_prev)
        def _():
            for copy in copies:
                copy.wait_recv()

        for lag in range(1, LAGS + 1):
            count = min(lag, frames)
            past = earlier[row, LAGS - lag : LAGS - lag + count, columns]
            term = dot(past.reshape(-1, channels), wtime[lag])
            for f in range(count):
                totals[f] += term[f * width : (f + 1) * width]
        for f in range(frames):
            temporal = totals[f].astype(jnp.bfloat16).astype(jnp.float32)
            kept = hidden[row, f, columns].astype(jnp.float32)
            out[f, row, columns] = (kept + temporal + vector(3)).astype(jnp.bfloat16)

    @pl.when(jnp.logical_not(has_prev))
    def _():
        earlier[...] = jnp.zeros_like(earlier)

    @pl.when(jnp.logical_not(has_up))
    def _():
        feat[0] = jnp.zeros(feat.shape[1:], feat.dtype)

    @pl.when(jnp.logical_not(has_down))
    def _():
        feat[rows + 1] = jnp.zeros(feat.shape[1:], feat.dtype)

    for i in (2, 3, 4, 5):
        weight_copies[i].wait()
    for row in range(3):
        row_copy(row).wait()
    for f in reversed(range(frames)):
        for side in range(2):
            part = (f, 1, side * half, half)
            for slot in range(first, first + 3):
                norm_part(slot, *part)
            if f == frames - 1 and side == 0:
                weight_copies[0].wait()
            space_part(first, *part)
            if f >= frames - LAGS:
                pl.when(has_next)(first_copies[f - frames + LAGS, side].start)

    @pl.loop(first + 1, last)
    def _(row):
        row_copy(row + 1).wait()
        norm_part(row + 2)
        space_row(row)

    pl.when(has_up)(to_down.wait_recv)
    pl.when(has_down)(to_up.wait_recv)
    norm_part(0)
    space_row(0)
    norm_part(rows + 1)
    space_part(last)

    @pl.when(has_next)
    def _():
        for copy in last_copies:
            copy.start()

    weight_copies[1].wait()
    time_part(first, first_copies.values())

    @pl.loop(first + 1, last)
    def _(row):
        time_part(row, [time_copy(row, row)])

    time_part(0, [time_copy(0, 0)])
    for side in range(2):
        time_part(last, [last_copies[side]], side * half, half)

    pl.when(has_up)(to_up.wait_send)
    pl.when(has_down)(to_down.wait_send)

    @pl.when(has_next)
    def _():
        for copy in (time_copy(0, 0), *first_copies.values(), *last_copies):
            copy.wait_send()

        @pl.loop(first + 1, last)
        def _(row):
            time_copy(row, row).wait_send()


def body(features, *rest):
    frames, rows, cols, channels = features.shape
    bf16 = jnp.bfloat16
    return pl.pallas_call(
        kernel,
        out_shape=jax.ShapeDtypeStruct(features.shape, bf16),
        in_specs=[pl.BlockSpec(memory_space=pltpu.HBM)] * 7,
        out_specs=pl.BlockSpec(memory_space=pltpu.VMEM),
        scratch_shapes=[
            pltpu.VMEM((rows + 2, frames, cols, channels), bf16),
            pltpu.VMEM((rows + 2, frames, cols, 3 * channels), bf16),
            pltpu.VMEM((rows, frames, cols, channels), bf16),
            pltpu.VMEM((rows, frames, cols, channels), bf16),
            pltpu.VMEM((rows, LAGS, cols, channels), bf16),
            pltpu.VMEM(rest[0].shape, bf16),
            pltpu.VMEM(rest[3].shape, bf16),
            pltpu.VMEM((4, channels), jnp.float32),
            pltpu.SemaphoreType.DMA((rows,)),
            pltpu.SemaphoreType.DMA((6,)),
            pltpu.SemaphoreType.DMA((2,)),
            pltpu.SemaphoreType.DMA((2,)),
            pltpu.SemaphoreType.DMA((rows + 2 * LAGS + 2,)),
            pltpu.SemaphoreType.DMA((rows + 2 * LAGS + 2,)),
        ],
        compiler_params=pltpu.CompilerParams(
            collective_id=0, has_side_effects=True, vmem_limit_bytes=36 * 1024 * 1024
        ),
    )(*[pltpu.with_memory_space_constraint(x, pltpu.HBM) for x in (features, *rest)])


def solution(mesh):
    return jax.shard_map(
        body,
        mesh=mesh,
        in_specs=(P(("grp", "frame"), "band", None, None), P(), P(), P(), P(), P(), P()),
        out_specs=P(("grp", "frame"), "band", None, None),
        check_vma=False,
    )
```

```python
import functools

import jax
import jax.numpy as jnp
from jax import lax
from jax.experimental import pallas as pl
from jax.experimental.pallas import tpu as pltpu
from jax.sharding import PartitionSpec as P

LAGS = 2


def rms_silu(values, gain):
    mean = jnp.mean(values * values, axis=-1, keepdims=True)
    half = values * lax.rsqrt(mean + 1e-06) * (0.5 * gain)
    return half + half * jnp.tanh(half)


def dot(left, right):
    return jnp.dot(left, right, preferred_element_type=jnp.float32)


def kernel(
    features, space_kernel, space_gain, space_bias, time_kernel, time_gain, time_bias,
    out,
    feat, normed, hidden, ntime, earlier, wspace, wtime, vectors,
    feat_sem, weight_sem, halo_send, halo_recv, time_send, time_recv,
):
    frames, rows, cols, channels = features.shape
    half = cols // 2
    last = rows - 1
    band, bands = lax.axis_index("band"), lax.axis_size("band")
    frame, frame_parts = lax.axis_index("frame"), lax.axis_size("frame")
    has_up, has_down = band > 0, band < bands - 1
    has_prev, has_next = frame > 0, frame < frame_parts - 1
    neighbours = (
        (has_up, {"band": band - 1}),
        (has_down, {"band": band + 1}),
        (has_prev, {"frame": frame - 1}),
        (has_next, {"frame": frame + 1}),
    )

    barrier = pltpu.get_barrier_semaphore()
    for present, device in neighbours:
        @pl.when(present)
        def _():
            pl.semaphore_signal(
                barrier, inc=1, device_id=device, device_id_type=pl.DeviceIdType.MESH
            )

    def row_copy(row):
        return pltpu.make_async_copy(
            features.at[:, row], feat.at[row + 1], feat_sem.at[row]
        )

    weights = [(space_kernel, wspace), (time_kernel, wtime)] + [
        (vector, vectors.at[i])
        for i, vector in enumerate((space_gain, space_bias, time_gain, time_bias))
    ]
    weight_copies = [
        pltpu.make_async_copy(source, target, weight_sem.at[i])
        for i, (source, target) in enumerate(weights)
    ]
    for i in (2, 3, 4, 5):
        weight_copies[i].start()
    for row in range(3):
        row_copy(row).start()
    weight_copies[0].start()
    for row in range(3, rows):
        row_copy(row).start()
    weight_copies[1].start()

    def time_copy(row, sem, start=0, count=LAGS, left=0, width=cols):
        return pltpu.make_async_remote_copy(
            ntime.at[row, pl.ds(frames - LAGS + start, count), pl.ds(left, width)],
            earlier.at[row, pl.ds(start, count), pl.ds(left, width)],
            time_send.at[sem],
            time_recv.at[sem],
            device_id={"frame": frame + 1},
            device_id_type=pl.DeviceIdType.MESH,
        )

    last_copies = [
        time_copy(last, rows + side, 0, LAGS, side * half, half)
        for side in range(2)
    ]

    def vector(i):
        return vectors[i].reshape(1, channels)

    def norm_part(slot, start=0, count=frames, left=0, width=cols):
        base = max(0, min(left - 16, cols - width - 16)) if width < cols else 0
        window = min(cols, width + 16)
        size = count * window
        values = feat[slot, start : start + count, base : base + window]
        result = rms_silu(values.reshape(size, channels).astype(jnp.float32), vector(0))
        column = base + lax.rem(
            lax.broadcasted_iota(jnp.int32, (size, channels), 0), window
        )
        before = jnp.where(column == 0, 0.0, pltpu.roll(result, 1, 0))
        after = jnp.where(column == cols - 1, 0.0, pltpu.roll(result, size - 1, 0))
        for i, piece in enumerate((before, result, after)):
            kept = piece.astype(jnp.bfloat16).reshape(count, window, channels)
            normed[
                slot, start : start + count, left : left + width,
                i * channels : (i + 1) * channels,
            ] = kept[:, left - base : left - base + width]

    def space_part(row, start=0, count=frames, left=0, width=cols):
        where = (slice(start, start + count), slice(left, left + width))
        size = count * width
        total = None
        for i in range(3):
            product = dot(
                normed[(row + i, *where)].reshape(size, 3 * channels),
                wspace[i].reshape(3 * channels, channels),
            )
            total = product if total is None else total + product
        centre = feat[(row + 1, *where)].reshape(size, channels).astype(jnp.float32)
        kept = (centre + total + vector(1)).astype(jnp.bfloat16)
        shape = (count, width, channels)
        hidden[(row, *where)] = kept.reshape(shape)
        ntime[(row, *where)] = (
            rms_silu(kept.astype(jnp.float32), vector(2)).astype(jnp.bfloat16).reshape(shape)
        )

    def space_row(row):
        space_part(row)
        pl.when(has_next)(time_copy(row, row).start)

    def time_part(row, copies, left=0, width=cols):
        columns = slice(left, left + width)
        own = ntime[row, :, columns]
        totals = [
            dot(own.reshape(-1, channels), wtime[0]).reshape(own.shape)[f]
            for f in range(frames)
        ]
        for lag in range(1, min(LAGS, frames - 1) + 1):
            term = dot(own[: frames - lag].reshape(-1, channels), wtime[lag])
            for f in range(lag, frames):
                totals[f] += term[(f - lag) * width : (f - lag + 1) * width]

        @pl.when(has_prev)
        def _():
            for copy in copies:
                copy.wait_recv()

        for lag in range(1, LAGS + 1):
            count = min(lag, frames)
            past = earlier[row, LAGS - lag : LAGS - lag + count, columns]
            term = dot(past.reshape(-1, channels), wtime[lag])
            for f in range(count):
                totals[f] += term[f * width : (f + 1) * width]
        for f in range(frames):
            temporal = totals[f].astype(jnp.bfloat16).astype(jnp.float32)
            kept = hidden[row, f, columns].astype(jnp.float32)
            out[f, row, columns] = (kept + temporal + vector(3)).astype(jnp.bfloat16)

    @pl.when(jnp.logical_not(has_prev))
    def _():
        earlier[...] = jnp.zeros_like(earlier)

    @pl.when(jnp.logical_not(has_up))
    def _():
        feat[0] = jnp.zeros(feat.shape[1:], feat.dtype)

    @pl.when(jnp.logical_not(has_down))
    def _():
        feat[rows + 1] = jnp.zeros(feat.shape[1:], feat.dtype)

    for i in (2, 3, 4, 5):
        weight_copies[i].wait()
    for row in range(3):
        row_copy(row).wait()
        norm_part(row + 1)

    peers = (
        (band + bands - 1) // bands
        + 1 - (band + 1) // bands
        + (frame + frame_parts - 1) // frame_parts
        + 1 - (frame + 1) // frame_parts
    )
    pl.semaphore_wait(barrier, peers)

    to_up = pltpu.make_async_remote_copy(
        features.at[:, 0], feat.at[rows + 1], halo_send.at[0], halo_recv.at[0],
        device_id={"band": band - 1}, device_id_type=pl.DeviceIdType.MESH,
    )
    to_down = pltpu.make_async_remote_copy(
        features.at[:, rows - 1], feat.at[0], halo_send.at[1], halo_recv.at[1],
        device_id={"band": band + 1}, device_id_type=pl.DeviceIdType.MESH,
    )
    pl.when(has_up)(to_up.start)
    pl.when(has_down)(to_down.start)

    weight_copies[0].wait()
    space_row(1)

    @pl.loop(2, last)
    def _(row):
        row_copy(row + 1).wait()
        norm_part(row + 2)
        space_row(row)

    pl.when(has_up)(to_down.wait_recv)
    pl.when(has_down)(to_up.wait_recv)
    norm_part(0)
    space_row(0)
    norm_part(rows + 1)
    space_part(last)

    @pl.when(has_next)
    def _():
        for copy in last_copies:
            copy.start()

    weight_copies[1].wait()
    @pl.loop(1, last)
    def _(row):
        time_part(row, [time_copy(row, row)])

    time_part(0, [time_copy(0, 0)])
    for side in range(2):
        time_part(last, [last_copies[side]], side * half, half)

    pl.when(has_up)(to_up.wait_send)
    pl.when(has_down)(to_down.wait_send)

    @pl.when(has_next)
    def _():
        for copy in (time_copy(0, 0), *last_copies):
            copy.wait_send()

        @pl.loop(1, last)
        def _(row):
            time_copy(row, row).wait_send()


def body(features, *rest):
    frames, rows, cols, channels = features.shape
    bf16 = jnp.bfloat16
    return pl.pallas_call(
        kernel,
        out_shape=jax.ShapeDtypeStruct(features.shape, bf16),
        in_specs=[pl.BlockSpec(memory_space=pltpu.HBM)] * 7,
        out_specs=pl.BlockSpec(memory_space=pltpu.VMEM),
        scratch_shapes=[
            pltpu.VMEM((rows + 2, frames, cols, channels), bf16),
            pltpu.VMEM((rows + 2, frames, cols, 3 * channels), bf16),
            pltpu.VMEM((rows, frames, cols, channels), bf16),
            pltpu.VMEM((rows, frames, cols, channels), bf16),
            pltpu.VMEM((rows, LAGS, cols, channels), bf16),
            pltpu.VMEM(rest[0].shape, bf16),
            pltpu.VMEM(rest[3].shape, bf16),
            pltpu.VMEM((4, channels), jnp.float32),
            pltpu.SemaphoreType.DMA((rows,)),
            pltpu.SemaphoreType.DMA((6,)),
            pltpu.SemaphoreType.DMA((2,)),
            pltpu.SemaphoreType.DMA((2,)),
            pltpu.SemaphoreType.DMA((rows + 2,)),
            pltpu.SemaphoreType.DMA((rows + 2,)),
        ],
        compiler_params=pltpu.CompilerParams(
            collective_id=0, has_side_effects=True, vmem_limit_bytes=36 * 1024 * 1024
        ),
    )(*[pltpu.with_memory_space_constraint(x, pltpu.HBM) for x in (features, *rest)])


def solution(mesh):
    return jax.shard_map(
        body,
        mesh=mesh,
        in_specs=(P(("grp", "frame"), "band", None, None), P(), P(), P(), P(), P(), P()),
        out_specs=P(("grp", "frame"), "band", None, None),
        check_vma=False,
    )
```

```python
import functools

import jax
import jax.numpy as jnp
from jax import lax
from jax.experimental import pallas as pl
from jax.experimental.pallas import tpu as pltpu
from jax.sharding import PartitionSpec as P

LAGS = 2


def rms_silu(values, gain):
    mean = jnp.mean(values * values, axis=-1, keepdims=True)
    half = values * lax.rsqrt(mean + 1e-06) * (0.5 * gain)
    return half + half * jnp.tanh(half)


def dot(left, right):
    return jnp.dot(left, right, preferred_element_type=jnp.float32)


def kernel(
    features, space_kernel, space_gain, space_bias, time_kernel, time_gain, time_bias,
    out,
    feat, normed, hidden, ntime, earlier, wspace, wtime, vectors,
    feat_sem, weight_sem, halo_send, halo_recv, time_send, time_recv,
):
    frames, rows, cols, channels = features.shape
    half = cols // 2
    last = rows - 1
    band, bands = lax.axis_index("band"), lax.axis_size("band")
    frame, frame_parts = lax.axis_index("frame"), lax.axis_size("frame")
    has_up, has_down = band > 0, band < bands - 1
    has_prev, has_next = frame > 0, frame < frame_parts - 1
    neighbours = (
        (has_up, {"band": band - 1}),
        (has_down, {"band": band + 1}),
        (has_prev, {"frame": frame - 1}),
        (has_next, {"frame": frame + 1}),
    )

    barrier = pltpu.get_barrier_semaphore()
    for present, device in neighbours:
        @pl.when(present)
        def _():
            pl.semaphore_signal(
                barrier, inc=1, device_id=device, device_id_type=pl.DeviceIdType.MESH
            )

    def row_copy(row):
        return pltpu.make_async_copy(
            features.at[:, row], feat.at[row + 1], feat_sem.at[row]
        )

    weights = [(space_kernel, wspace), (time_kernel, wtime)] + [
        (vector, vectors.at[i])
        for i, vector in enumerate((space_gain, space_bias, time_gain, time_bias))
    ]
    weight_copies = [
        pltpu.make_async_copy(source, target, weight_sem.at[i])
        for i, (source, target) in enumerate(weights)
    ]
    for i in (2, 3, 4, 5):
        weight_copies[i].start()
    for row in range(3):
        row_copy(row).start()
    weight_copies[0].start()

    def time_copy(row, sem, start=0, count=LAGS, left=0, width=cols):
        return pltpu.make_async_remote_copy(
            ntime.at[row, pl.ds(frames - LAGS + start, count), pl.ds(left, width)],
            earlier.at[row, pl.ds(start, count), pl.ds(left, width)],
            time_send.at[sem],
            time_recv.at[sem],
            device_id={"frame": frame + 1},
            device_id_type=pl.DeviceIdType.MESH,
        )

    last_copies = [
        time_copy(last, rows + side, 0, LAGS, side * half, half)
        for side in range(2)
    ]

    def vector(i):
        return vectors[i].reshape(1, channels)

    def norm_part(slot, start=0, count=frames, left=0, width=cols):
        base = max(0, min(left - 16, cols - width - 16)) if width < cols else 0
        window = min(cols, width + 16)
        size = count * window
        values = feat[slot, start : start + count, base : base + window]
        result = rms_silu(values.reshape(size, channels).astype(jnp.float32), vector(0))
        column = base + lax.rem(
            lax.broadcasted_iota(jnp.int32, (size, channels), 0), window
        )
        before = jnp.where(column == 0, 0.0, pltpu.roll(result, 1, 0))
        after = jnp.where(column == cols - 1, 0.0, pltpu.roll(result, size - 1, 0))
        for i, piece in enumerate((before, result, after)):
            kept = piece.astype(jnp.bfloat16).reshape(count, window, channels)
            normed[
                slot, start : start + count, left : left + width,
                i * channels : (i + 1) * channels,
            ] = kept[:, left - base : left - base + width]

    def space_part(row, start=0, count=frames, left=0, width=cols):
        where = (slice(start, start + count), slice(left, left + width))
        size = count * width
        total = None
        for i in range(3):
            product = dot(
                normed[(row + i, *where)].reshape(size, 3 * channels),
                wspace[i].reshape(3 * channels, channels),
            )
            total = product if total is None else total + product
        centre = feat[(row + 1, *where)].reshape(size, channels).astype(jnp.float32)
        kept = (centre + total + vector(1)).astype(jnp.bfloat16)
        shape = (count, width, channels)
        hidden[(row, *where)] = kept.reshape(shape)
        ntime[(row, *where)] = (
            rms_silu(kept.astype(jnp.float32), vector(2)).astype(jnp.bfloat16).reshape(shape)
        )

    def space_row(row):
        space_part(row)
        pl.when(has_next)(time_copy(row, row).start)

    def time_part(row, copies, left=0, width=cols):
        columns = slice(left, left + width)
        own = ntime[row, :, columns]
        totals = [
            dot(own.reshape(-1, channels), wtime[0]).reshape(own.shape)[f]
            for f in range(frames)
        ]
        for lag in range(1, min(LAGS, frames - 1) + 1):
            term = dot(own[: frames - lag].reshape(-1, channels), wtime[lag])
            for f in range(lag, frames):
                totals[f] += term[(f - lag) * width : (f - lag + 1) * width]

        @pl.when(has_prev)
        def _():
            for copy in copies:
                copy.wait_recv()

        for lag in range(1, LAGS + 1):
            count = min(lag, frames)
            past = earlier[row, LAGS - lag : LAGS - lag + count, columns]
            term = dot(past.reshape(-1, channels), wtime[lag])
            for f in range(count):
                totals[f] += term[f * width : (f + 1) * width]
        for f in range(frames):
            temporal = totals[f].astype(jnp.bfloat16).astype(jnp.float32)
            kept = hidden[row, f, columns].astype(jnp.float32)
            out[f, row, columns] = (kept + temporal + vector(3)).astype(jnp.bfloat16)

    @pl.when(jnp.logical_not(has_prev))
    def _():
        earlier[...] = jnp.zeros_like(earlier)

    @pl.when(jnp.logical_not(has_up))
    def _():
        feat[0] = jnp.zeros(feat.shape[1:], feat.dtype)

    @pl.when(jnp.logical_not(has_down))
    def _():
        feat[rows + 1] = jnp.zeros(feat.shape[1:], feat.dtype)

    for i in (2, 3, 4, 5):
        weight_copies[i].wait()
    for row in range(3):
        row_copy(row).wait()
        norm_part(row + 1)

    peers = (
        (band + bands - 1) // bands
        + 1 - (band + 1) // bands
        + (frame + frame_parts - 1) // frame_parts
        + 1 - (frame + 1) // frame_parts
    )
    pl.semaphore_wait(barrier, peers)

    to_up = pltpu.make_async_remote_copy(
        features.at[:, 0], feat.at[rows + 1], halo_send.at[0], halo_recv.at[0],
        device_id={"band": band - 1}, device_id_type=pl.DeviceIdType.MESH,
    )
    to_down = pltpu.make_async_remote_copy(
        features.at[:, rows - 1], feat.at[0], halo_send.at[1], halo_recv.at[1],
        device_id={"band": band + 1}, device_id_type=pl.DeviceIdType.MESH,
    )
    pl.when(has_up)(to_up.start)
    pl.when(has_down)(to_down.start)

    for row in range(3, rows):
        row_copy(row).start()
    weight_copies[1].start()
    weight_copies[0].wait()
    space_row(1)

    @pl.loop(2, last)
    def _(row):
        row_copy(row + 1).wait()
        norm_part(row + 2)
        space_row(row)

    pl.when(has_up)(to_down.wait_recv)
    pl.when(has_down)(to_up.wait_recv)
    norm_part(0)
    space_row(0)
    norm_part(rows + 1)
    space_part(last)

    @pl.when(has_next)
    def _():
        for copy in last_copies:
            copy.start()

    weight_copies[1].wait()
    @pl.loop(1, last)
    def _(row):
        time_part(row, [time_copy(row, row)])

    time_part(0, [time_copy(0, 0)])
    time_part(last, last_copies)

    pl.when(has_up)(to_up.wait_send)
    pl.when(has_down)(to_down.wait_send)

    @pl.when(has_next)
    def _():
        for copy in (time_copy(0, 0), *last_copies):
            copy.wait_send()

        @pl.loop(1, last)
        def _(row):
            time_copy(row, row).wait_send()


def body(features, *rest):
    frames, rows, cols, channels = features.shape
    bf16 = jnp.bfloat16
    return pl.pallas_call(
        kernel,
        out_shape=jax.ShapeDtypeStruct(features.shape, bf16),
        in_specs=[pl.BlockSpec(memory_space=pltpu.HBM)] * 7,
        out_specs=pl.BlockSpec(memory_space=pltpu.VMEM),
        scratch_shapes=[
            pltpu.VMEM((rows + 2, frames, cols, channels), bf16),
            pltpu.VMEM((rows + 2, frames, cols, 3 * channels), bf16),
            pltpu.VMEM((rows, frames, cols, channels), bf16),
            pltpu.VMEM((rows, frames, cols, channels), bf16),
            pltpu.VMEM((rows, LAGS, cols, channels), bf16),
            pltpu.VMEM(rest[0].shape, bf16),
            pltpu.VMEM(rest[3].shape, bf16),
            pltpu.VMEM((4, channels), jnp.float32),
            pltpu.SemaphoreType.DMA((rows,)),
            pltpu.SemaphoreType.DMA((6,)),
            pltpu.SemaphoreType.DMA((2,)),
            pltpu.SemaphoreType.DMA((2,)),
            pltpu.SemaphoreType.DMA((rows + 2,)),
            pltpu.SemaphoreType.DMA((rows + 2,)),
        ],
        compiler_params=pltpu.CompilerParams(
            collective_id=0, has_side_effects=True, vmem_limit_bytes=36 * 1024 * 1024
        ),
    )(*[pltpu.with_memory_space_constraint(x, pltpu.HBM) for x in (features, *rest)])


def solution(mesh):
    return jax.shard_map(
        body,
        mesh=mesh,
        in_specs=(P(("grp", "frame"), "band", None, None), P(), P(), P(), P(), P(), P()),
        out_specs=P(("grp", "frame"), "band", None, None),
        check_vma=False,
    )
```

```python
import functools

import jax
import jax.numpy as jnp
from jax import lax
from jax.experimental import pallas as pl
from jax.experimental.pallas import tpu as pltpu
from jax.sharding import PartitionSpec as P

LAGS = 2


def rms_silu(values, gain):
    mean = jnp.mean(values * values, axis=-1, keepdims=True)
    half = values * lax.rsqrt(mean + 1e-06) * (0.5 * gain)
    return half + half * jnp.tanh(half)


def dot(left, right):
    return jnp.dot(left, right, preferred_element_type=jnp.float32)


def kernel(
    features, space_kernel, space_gain, space_bias, time_kernel, time_gain, time_bias,
    out,
    feat, normed, hidden, ntime, earlier, wspace, wtime, vectors,
    feat_sem, weight_sem, halo_send, halo_recv, time_send, time_recv,
):
    frames, rows, cols, channels = features.shape
    half = cols // 2
    last = rows - 1
    band, bands = lax.axis_index("band"), lax.axis_size("band")
    frame, frame_parts = lax.axis_index("frame"), lax.axis_size("frame")
    has_up, has_down = band > 0, band < bands - 1
    has_prev, has_next = frame > 0, frame < frame_parts - 1
    neighbours = (
        (has_up, {"band": band - 1}),
        (has_down, {"band": band + 1}),
        (has_prev, {"frame": frame - 1}),
        (has_next, {"frame": frame + 1}),
    )

    barrier = pltpu.get_barrier_semaphore()
    for present, device in neighbours:
        @pl.when(present)
        def _():
            pl.semaphore_signal(
                barrier, inc=1, device_id=device, device_id_type=pl.DeviceIdType.MESH
            )

    def row_copy(row):
        return pltpu.make_async_copy(
            features.at[:, row], feat.at[row + 1], feat_sem.at[row]
        )

    weights = [(space_kernel, wspace), (time_kernel, wtime)] + [
        (vector, vectors.at[i])
        for i, vector in enumerate((space_gain, space_bias, time_gain, time_bias))
    ]
    weight_copies = [
        pltpu.make_async_copy(source, target, weight_sem.at[i])
        for i, (source, target) in enumerate(weights)
    ]
    for i in (2, 3, 4, 5):
        weight_copies[i].start()
    for row in range(3):
        row_copy(row).start()
    weight_copies[0].start()

    def time_copy(row, sem, start=0, count=LAGS, left=0, width=cols):
        return pltpu.make_async_remote_copy(
            ntime.at[row, pl.ds(frames - LAGS + start, count), pl.ds(left, width)],
            earlier.at[row, pl.ds(start, count), pl.ds(left, width)],
            time_send.at[sem],
            time_recv.at[sem],
            device_id={"frame": frame + 1},
            device_id_type=pl.DeviceIdType.MESH,
        )

    first_copies = [
        time_copy(1, rows + 2 + start, start, 1) for start in range(LAGS)
    ]
    last_copies = [
        time_copy(last, rows + side, 0, LAGS, side * half, half)
        for side in range(2)
    ]

    def vector(i):
        return vectors[i].reshape(1, channels)

    def norm_part(slot, start=0, count=frames, left=0, width=cols):
        base = max(0, min(left - 16, cols - width - 16)) if width < cols else 0
        window = min(cols, width + 16)
        size = count * window
        values = feat[slot, start : start + count, base : base + window]
        result = rms_silu(values.reshape(size, channels).astype(jnp.float32), vector(0))
        column = base + lax.rem(
            lax.broadcasted_iota(jnp.int32, (size, channels), 0), window
        )
        before = jnp.where(column == 0, 0.0, pltpu.roll(result, 1, 0))
        after = jnp.where(column == cols - 1, 0.0, pltpu.roll(result, size - 1, 0))
        for i, piece in enumerate((before, result, after)):
            kept = piece.astype(jnp.bfloat16).reshape(count, window, channels)
            normed[
                slot, start : start + count, left : left + width,
                i * channels : (i + 1) * channels,
            ] = kept[:, left - base : left - base + width]

    def space_part(row, start=0, count=frames, left=0, width=cols):
        where = (slice(start, start + count), slice(left, left + width))
        size = count * width
        total = None
        for i in range(3):
            product = dot(
                normed[(row + i, *where)].reshape(size, 3 * channels),
                wspace[i].reshape(3 * channels, channels),
            )
            total = product if total is None else total + product
        centre = feat[(row + 1, *where)].reshape(size, channels).astype(jnp.float32)
        kept = (centre + total + vector(1)).astype(jnp.bfloat16)
        shape = (count, width, channels)
        hidden[(row, *where)] = kept.reshape(shape)
        ntime[(row, *where)] = (
            rms_silu(kept.astype(jnp.float32), vector(2)).astype(jnp.bfloat16).reshape(shape)
        )

    def space_row(row):
        space_part(row)
        pl.when(has_next)(time_copy(row, row).start)

    def time_part(row, copies, left=0, width=cols):
        columns = slice(left, left + width)
        own = ntime[row, :, columns]
        totals = [
            dot(own.reshape(-1, channels), wtime[0]).reshape(own.shape)[f]
            for f in range(frames)
        ]
        for lag in range(1, min(LAGS, frames - 1) + 1):
            term = dot(own[: frames - lag].reshape(-1, channels), wtime[lag])
            for f in range(lag, frames):
                totals[f] += term[(f - lag) * width : (f - lag + 1) * width]

        @pl.when(has_prev)
        def _():
            for copy in copies:
                copy.wait_recv()

        for lag in range(1, LAGS + 1):
            count = min(lag, frames)
            past = earlier[row, LAGS - lag : LAGS - lag + count, columns]
            term = dot(past.reshape(-1, channels), wtime[lag])
            for f in range(count):
                totals[f] += term[f * width : (f + 1) * width]
        for f in range(frames):
            temporal = totals[f].astype(jnp.bfloat16).astype(jnp.float32)
            kept = hidden[row, f, columns].astype(jnp.float32)
            out[f, row, columns] = (kept + temporal + vector(3)).astype(jnp.bfloat16)

    @pl.when(jnp.logical_not(has_prev))
    def _():
        earlier[...] = jnp.zeros_like(earlier)

    @pl.when(jnp.logical_not(has_up))
    def _():
        feat[0] = jnp.zeros(feat.shape[1:], feat.dtype)

    @pl.when(jnp.logical_not(has_down))
    def _():
        feat[rows + 1] = jnp.zeros(feat.shape[1:], feat.dtype)

    for i in (2, 3, 4, 5):
        weight_copies[i].wait()
    for row in range(3):
        row_copy(row).wait()
        norm_part(row + 1)

    peers = (
        (band + bands - 1) // bands
        + 1 - (band + 1) // bands
        + (frame + frame_parts - 1) // frame_parts
        + 1 - (frame + 1) // frame_parts
    )
    pl.semaphore_wait(barrier, peers)

    to_up = pltpu.make_async_remote_copy(
        features.at[:, 0], feat.at[rows + 1], halo_send.at[0], halo_recv.at[0],
        device_id={"band": band - 1}, device_id_type=pl.DeviceIdType.MESH,
    )
    to_down = pltpu.make_async_remote_copy(
        features.at[:, rows - 1], feat.at[0], halo_send.at[1], halo_recv.at[1],
        device_id={"band": band + 1}, device_id_type=pl.DeviceIdType.MESH,
    )
    pl.when(has_up)(to_up.start)
    pl.when(has_down)(to_down.start)

    for row in range(3, rows):
        row_copy(row).start()
    weight_copies[1].start()
    weight_copies[0].wait()
    for start in reversed(range(frames)):
        space_part(1, start, 1)
        if start >= frames - LAGS:
            pl.when(has_next)(first_copies[start - frames + LAGS].start)

    @pl.loop(2, last)
    def _(row):
        row_copy(row + 1).wait()
        norm_part(row + 2)
        space_row(row)

    pl.when(has_up)(to_down.wait_recv)
    pl.when(has_down)(to_up.wait_recv)
    norm_part(0)
    space_row(0)
    norm_part(rows + 1)
    space_part(last)

    @pl.when(has_next)
    def _():
        for copy in last_copies:
            copy.start()

    weight_copies[1].wait()
    time_part(1, first_copies)

    @pl.loop(2, last)
    def _(row):
        time_part(row, [time_copy(row, row)])

    time_part(0, [time_copy(0, 0)])
    time_part(last, last_copies)

    pl.when(has_up)(to_up.wait_send)
    pl.when(has_down)(to_down.wait_send)

    @pl.when(has_next)
    def _():
        for copy in (time_copy(0, 0), *first_copies, *last_copies):
            copy.wait_send()

        @pl.loop(2, last)
        def _(row):
            time_copy(row, row).wait_send()


def body(features, *rest):
    frames, rows, cols, channels = features.shape
    bf16 = jnp.bfloat16
    return pl.pallas_call(
        kernel,
        out_shape=jax.ShapeDtypeStruct(features.shape, bf16),
        in_specs=[pl.BlockSpec(memory_space=pltpu.HBM)] * 7,
        out_specs=pl.BlockSpec(memory_space=pltpu.VMEM),
        scratch_shapes=[
            pltpu.VMEM((rows + 2, frames, cols, channels), bf16),
            pltpu.VMEM((rows + 2, frames, cols, 3 * channels), bf16),
            pltpu.VMEM((rows, frames, cols, channels), bf16),
            pltpu.VMEM((rows, frames, cols, channels), bf16),
            pltpu.VMEM((rows, LAGS, cols, channels), bf16),
            pltpu.VMEM(rest[0].shape, bf16),
            pltpu.VMEM(rest[3].shape, bf16),
            pltpu.VMEM((4, channels), jnp.float32),
            pltpu.SemaphoreType.DMA((rows,)),
            pltpu.SemaphoreType.DMA((6,)),
            pltpu.SemaphoreType.DMA((2,)),
            pltpu.SemaphoreType.DMA((2,)),
            pltpu.SemaphoreType.DMA((rows + 2 + LAGS,)),
            pltpu.SemaphoreType.DMA((rows + 2 + LAGS,)),
        ],
        compiler_params=pltpu.CompilerParams(
            collective_id=0, has_side_effects=True, vmem_limit_bytes=36 * 1024 * 1024
        ),
    )(*[pltpu.with_memory_space_constraint(x, pltpu.HBM) for x in (features, *rest)])


def solution(mesh):
    return jax.shard_map(
        body,
        mesh=mesh,
        in_specs=(P(("grp", "frame"), "band", None, None), P(), P(), P(), P(), P(), P()),
        out_specs=P(("grp", "frame"), "band", None, None),
        check_vma=False,
    )
```
